128 devices in a mesh: ctx: 16 (over z, y), head: 8 (over x, core).
Axes of the slice: x: 4, y: 4, z: 4, core: 2. Of those that a mesh axis runs over, the one named last changes fastest.
Arguments:
- queries: bfloat16 [8192, 4096], P('ctx', 'head'), may hold values from -160 to 160
- key_states: bfloat16 [8192, 4096], P('ctx', 'head'), may hold values from -160 to 160
- values: bfloat16 [8192, 4096], P('ctx', 'head'), may hold values from -6 to 6
- query_gain: bfloat16 [4096], P('head'), may hold values from 0.25 to 1.75
- key_gain: bfloat16 [4096], P('head'), may hold values from 0.25 to 1.75
- memory_blocks: int32 [16, 8], replicated, may hold values from 0 to 63, as said below
- cotangent: bfloat16 [8192, 4096], P('ctx', 'head'), may hold values from -6 to 6
Outputs:
- attended: bfloat16 [8192, 4096], P('ctx', 'head')
- query_grads: bfloat16 [8192, 4096], P('ctx', 'head')
- key_grads: bfloat16 [8192, 4096], P('ctx', 'head')
- value_grads: bfloat16 [8192, 4096], P('ctx', 'head')
The draws below stay inside these ranges and needn't reach their ends.
Inputs may be any that keep to these rules, and one draw needn't show every extreme that they name: `memory_blocks`: row c lists the 8 blocks read by the tokens of ctx index c; block b holds tokens 128 b to 128 b + 127, and the 8 blocks of one row lie on 8 different ctx indices.
All inputs are finite; a program needn't handle non-finite values.
Results may differ from the reference program's by a relative error of at most 0.0045.
The reference program's roundings to bfloat16 on the way count: a program that leaves them out, or rounds other values in their place, can miss the bound.
Values may be sent and summed in bfloat16 or wider, within the bound.
No kernel may reach another device: no remote copies, remote signals or barrier semaphores. Data moves between devices by JAX's collectives and lax.ppermute only.
A program may use at most 128 MiB of HBM per device.

```python
import math
from functools import partial
import jax
import jax.numpy as jnp
from jax import lax

HEADS = 32
DH = 128
D = 4096
SEG = 512
LEVELS = 4
BLOCK = 128
NB = 8
TOKENS = 8192


def feature_scales(base_key, slope_value):
    position = (jnp.arange(HEADS * DH) // DH).astype(jnp.float32) / max(HEADS - 1, 1)
    jitter = jax.random.uniform(base_key, (HEADS * DH,), jnp.float32, -0.5, 0.5)
    return jnp.exp(slope_value * position + jitter)


def token_scales(base_key):
    return jnp.exp(jax.random.uniform(base_key, (TOKENS,), jnp.float32, math.log(0.3), math.log(3.0)))


def draw_pair(key):
    key_list = jax.random.split(jax.random.fold_in(key, 4242), 8)
    width_all = HEADS * DH
    slope_value = math.log(3.0)
    raw_query = jnp.clip(jax.random.normal(key_list[2], (TOKENS, width_all), jnp.float32), -4.0, 4.0)
    raw_key = jnp.clip(jax.random.normal(key_list[3], (TOKENS, width_all), jnp.float32), -4.0, 4.0)
    query_array = raw_query * token_scales(key_list[4])[:, None] * feature_scales(key_list[5], slope_value)[None, :]
    key_array = raw_key * token_scales(key_list[6])[:, None] * feature_scales(key_list[7], slope_value)[None, :]
    return (query_array, key_array)


def draw_queries(key, part):
    return draw_pair(key)[0].astype(jnp.bfloat16)


def draw_key_states(key, part):
    return draw_pair(key)[1].astype(jnp.bfloat16)


def put_first(row_values, target):
    position = jnp.argmax(row_values == target)
    return row_values.at[position].set(row_values[0]).at[0].set(target)


def draw_memory_blocks(key, part):
    reader_count = TOKENS // SEG
    block_count = SEG // BLOCK
    first_key, second_key = jax.random.split(jax.random.fold_in(key, 77))
    row_keys = jax.random.split(first_key, reader_count)

    def one_row(row_key):
        return jax.random.permutation(row_key, reader_count).astype(jnp.int32)
    owners = jax.vmap(one_row)(row_keys)
    owners = owners.at[0].set(put_first(owners[0], reader_count - 1))
    owners = owners.at[1].set(put_first(owners[1], 0))
    local_ids = jax.random.randint(second_key, (reader_count, NB), 0, block_count).astype(jnp.int32)
    local_ids = local_ids.at[0, 0].set(block_count - 1).at[1, 0].set(0)
    return (owners[:, :NB] * block_count + local_ids).astype(jnp.int32)


def levels(own_key, dims, cuts, smallest, top_value):
    factor_of = 1.0
    for dim, shards_of in cuts:
        heights = jax.random.uniform(jax.random.fold_in(jax.random.fold_in(own_key, 6), dim), (shards_of,), jnp.float32, smallest / len(cuts), top_value / len(cuts))
        factor_of = factor_of * jnp.repeat(jnp.exp(heights), dims[dim] // shards_of).reshape((-1,) + (1,) * (len(dims) - 1 - dim))
    return factor_of


def normal_values(key, shape, spread, limit, cuts=(), kind=jnp.bfloat16):
    drawn = spread * jax.random.normal(key, shape, jnp.float32)
    if cuts:
        drawn = drawn * levels(key, shape, cuts, -0.22, 0.18)
    return jnp.clip(drawn, -limit, limit).astype(kind)


def setup_inputs(seed: int = 0) -> dict:
    splits = jax.random.split(jax.random.key(seed), 8)
    queries = draw_queries(jax.random.fold_in(splits[7], 71), 0)
    key_states = draw_key_states(jax.random.fold_in(splits[7], 71), 0)
    values = normal_values(splits[2], (TOKENS, D), 1.0, 6.0, ((0, 16), (1, 8)))
    query_gain = jnp.clip(1.0 + 0.15 * jax.random.normal(splits[3], (D,), jnp.float32), 0.25, 1.75).astype(jnp.bfloat16)
    key_gain = jnp.clip(1.0 + 0.15 * jax.random.normal(splits[4], (D,), jnp.float32), 0.25, 1.75).astype(jnp.bfloat16)
    memory_blocks = draw_memory_blocks(jax.random.fold_in(splits[7], 71), 0)
    cotangent = normal_values(splits[6], (TOKENS, D), 1.0, 6.0, ((0, 16), (1, 8)))
    return {"queries": queries, "key_states": key_states, "values": values, "query_gain": query_gain, "key_gain": key_gain, "memory_blocks": memory_blocks, "cotangent": cotangent}


EPSILON = 1e-06
FLOOR_SCORE = -1e+30

def round_trip(array):
    return lax.optimization_barrier(array.astype(jnp.bfloat16)).astype(jnp.float32)

def take_level(array, seg_count, stride, offset):
    shaped = array.reshape((seg_count, SEG, stride) + array.shape[1:])
    return lax.dynamic_index_in_dim(shaped, offset, 2, keepdims=False)

def put_level(block_values, seg_count, stride, offset, fill):
    filled = jnp.full((seg_count, SEG, stride) + block_values.shape[2:], fill, block_values.dtype)
    filled = lax.dynamic_update_slice_in_dim(filled, block_values[:, :, None], offset, 2)
    return filled.reshape((TOKENS,) + block_values.shape[2:])

def forward_block(query_rows, key_rows, value_rows, score_scale):
    scores = jnp.einsum('nqd,nkd->nqk', query_rows.astype(jnp.float32), key_rows.astype(jnp.float32)) * score_scale
    row_max = lax.optimization_barrier(jnp.max(scores, axis=2))
    weights = jnp.exp(scores - row_max[:, :, None])
    row_total = lax.optimization_barrier(jnp.sum(weights, axis=2))
    summed = jnp.einsum('nqk,nkd->nqd', round_trip(weights), value_rows.astype(jnp.float32))
    return (row_max, row_total, summed)

def backward_block(query_rows, key_rows, value_rows, grad_rows, log_sum, delta_rows, score_scale):
    scores = jnp.einsum('nqd,nkd->nqk', query_rows.astype(jnp.float32), key_rows.astype(jnp.float32)) * score_scale
    softmax_rows = jnp.exp(scores - log_sum[:, :, None])
    grad_softmax = jnp.einsum('nqd,nkd->nqk', grad_rows.astype(jnp.float32), value_rows.astype(jnp.float32))
    grad_scores = round_trip(softmax_rows * (grad_softmax - delta_rows[:, :, None]))
    grad_query = jnp.einsum('nqk,nkd->nqd', grad_scores, key_rows.astype(jnp.float32)) * score_scale
    grad_key = jnp.einsum('nqk,nqd->nkd', grad_scores, query_rows.astype(jnp.float32)) * score_scale
    grad_value = jnp.einsum('nqk,nqd->nkd', round_trip(softmax_rows), grad_rows.astype(jnp.float32))
    return (grad_query, grad_key, grad_value)

def head_pass(head_index, query_head, key_head, value_head, grad_head, memory_blocks, score_scale):
    reader_count = TOKENS // SEG
    block_total = TOKENS // BLOCK
    layouts = []
    for level_index in range(LEVELS):
        stride = 2 ** level_index
        layouts.append((TOKENS // (SEG * stride), stride, head_index % stride))
    part_max = []
    part_total = []
    part_sum = []
    for seg_count, stride, offset in layouts:
        take_rows = partial(take_level, seg_count=seg_count, stride=stride, offset=offset)
        row_max, row_total, summed = forward_block(take_rows(query_head), take_rows(key_head), take_rows(value_head), score_scale)
        part_max.append(put_level(row_max, seg_count, stride, offset, FLOOR_SCORE))
        part_total.append(put_level(row_total, seg_count, stride, offset, 0.0))
        part_sum.append(put_level(summed, seg_count, stride, offset, 0.0))
    memory_keys = key_head.reshape(block_total, BLOCK, DH)[memory_blocks].reshape(reader_count, NB * BLOCK, DH)
    memory_values = value_head.reshape(block_total, BLOCK, DH)[memory_blocks].reshape(reader_count, NB * BLOCK, DH)
    memory_queries = query_head.reshape(reader_count, SEG, DH)
    row_max, row_total, summed = forward_block(memory_queries, memory_keys, memory_values, score_scale)
    part_max.append(row_max.reshape(TOKENS))
    part_total.append(row_total.reshape(TOKENS))
    part_sum.append(summed.reshape(TOKENS, DH))
    joint_max = lax.optimization_barrier(jnp.max(jnp.stack(part_max), axis=0))
    joint_total = jnp.zeros((TOKENS,), jnp.float32)
    numerator = jnp.zeros((TOKENS, DH), jnp.float32)
    for part_index in range(len(part_max)):
        factor = jnp.exp(part_max[part_index] - joint_max)
        joint_total = joint_total + factor * part_total[part_index]
        numerator = numerator + factor[:, None] * part_sum[part_index]
    merged = numerator / joint_total[:, None]
    log_sum = joint_max + jnp.log(joint_total)
    delta_full = lax.optimization_barrier(jnp.sum(grad_head.astype(jnp.float32) * merged, axis=1))
    grad_query_total = jnp.zeros((TOKENS, DH), jnp.float32)
    grad_key_total = jnp.zeros((TOKENS, DH), jnp.float32)
    grad_value_total = jnp.zeros((TOKENS, DH), jnp.float32)
    for seg_count, stride, offset in layouts:
        take_rows = partial(take_level, seg_count=seg_count, stride=stride, offset=offset)
        grad_query, grad_key, grad_value = backward_block(take_rows(query_head), take_rows(key_head), take_rows(value_head), take_rows(grad_head), take_rows(log_sum), take_rows(delta_full), score_scale)
        grad_query_total = grad_query_total + put_level(grad_query, seg_count, stride, offset, 0.0)
        grad_key_total = grad_key_total + put_level(grad_key, seg_count, stride, offset, 0.0)
        grad_value_total = grad_value_total + put_level(grad_value, seg_count, stride, offset, 0.0)
    grad_query, grad_key, grad_value = backward_block(memory_queries, memory_keys, memory_values, grad_head.reshape(reader_count, SEG, DH), log_sum.reshape(reader_count, SEG), delta_full.reshape(reader_count, SEG), score_scale)
    grad_query_total = grad_query_total + grad_query.reshape(TOKENS, DH)
    key_back = jnp.zeros((block_total, BLOCK, DH), jnp.float32).at[memory_blocks].add(round_trip(grad_key).reshape(reader_count, NB, BLOCK, DH))
    value_back = jnp.zeros((block_total, BLOCK, DH), jnp.float32).at[memory_blocks].add(round_trip(grad_value).reshape(reader_count, NB, BLOCK, DH))
    grad_key_total = grad_key_total + key_back.reshape(TOKENS, DH)
    grad_value_total = grad_value_total + value_back.reshape(TOKENS, DH)
    return (merged, grad_query_total, grad_key_total, grad_value_total)

def reference(queries, key_states, values, query_gain, key_gain, memory_blocks, cotangent):
    score_scale = 1.0 / math.sqrt(DH)
    query_float = queries.astype(jnp.float32)
    key_float = key_states.astype(jnp.float32)
    query_inverse = lax.rsqrt(lax.optimization_barrier(jnp.mean(query_float * query_float, axis=1, keepdims=True)) + EPSILON)
    key_inverse = lax.rsqrt(lax.optimization_barrier(jnp.mean(key_float * key_float, axis=1, keepdims=True)) + EPSILON)
    query_normed = (query_float * query_inverse * query_gain.astype(jnp.float32)).astype(jnp.bfloat16)
    key_normed = (key_float * key_inverse * key_gain.astype(jnp.float32)).astype(jnp.bfloat16)

    def split_heads(array):
        return array.reshape(TOKENS, HEADS, DH).transpose(1, 0, 2)

    def join_heads(array):
        return array.transpose(1, 0, 2).reshape(TOKENS, HEADS * DH)

    def one_head(head_item):
        head_index, query_head, key_head, value_head, grad_head = head_item
        return head_pass(head_index, query_head, key_head, value_head, grad_head, memory_blocks, score_scale)
    merged, grad_query_normed, grad_key_normed, grad_value = lax.map(one_head, (jnp.arange(HEADS, dtype=jnp.int32), split_heads(query_normed), split_heads(key_normed), split_heads(values), split_heads(cotangent)))
    attended = join_heads(merged).astype(jnp.bfloat16)
    query_adjoint = query_gain.astype(jnp.float32) * join_heads(grad_query_normed)
    key_adjoint = key_gain.astype(jnp.float32) * join_heads(grad_key_normed)
    query_inner = lax.optimization_barrier(jnp.sum(query_float * query_adjoint, axis=1, keepdims=True))
    key_inner = lax.optimization_barrier(jnp.sum(key_float * key_adjoint, axis=1, keepdims=True))
    query_grads = (query_inverse * query_adjoint - query_float * query_inverse ** 3 * query_inner / (HEADS * DH)).astype(jnp.bfloat16)
    key_grads = (key_inverse * key_adjoint - key_float * key_inverse ** 3 * key_inner / (HEADS * DH)).astype(jnp.bfloat16)
    value_grads = join_heads(grad_value).astype(jnp.bfloat16)
    return (attended, query_grads, key_grads, value_grads)
```

```python
import math

import jax
import jax.numpy as jnp
from jax import lax
from jax.experimental import pallas as pl
from jax.experimental.pallas import tpu as pltpu
from jax.sharding import Mesh
from jax.sharding import PartitionSpec as P

DH = 128
D = 4096
SEG = 512
EPSILON = 1e-06
FLOOR = -1e30
SCALE = 1.0 / math.sqrt(DH)
F32 = jnp.float32
BF16 = jnp.bfloat16


def nt(a, b):
    return lax.dot_general(a, b, (((1,), (1,)), ((), ())), preferred_element_type=F32)


def nn(a, b):
    return lax.dot_general(a, b, (((1,), (0,)), ((), ())), preferred_element_type=F32)


def tn(a, b):
    return lax.dot_general(a, b, (((0,), (0,)), ((), ())), preferred_element_type=F32)


def order_matrix(transposed):
    row = lax.broadcasted_iota(jnp.int32, (SEG, SEG), 1 if transposed else 0)
    col = lax.broadcasted_iota(jnp.int32, (SEG, SEG), 0 if transposed else 1)
    rb = row >> 6
    residue = ((rb & 1) << 2) | (rb & 2) | (rb >> 2)
    return (col == ((row & 63) * 8 + residue)).astype(F32).astype(BF16)


def slab(index):
    return pl.ds(pl.multiple_of(index * DH, DH), DH)


SMEM = pl.BlockSpec(memory_space=pltpu.SMEM)
VM = pl.BlockSpec(memory_space=pltpu.VMEM)


def call(body, ins, smem, outs, scratch=(), flops=0, name=None):
    return pl.pallas_call(
        body,
        out_shape=outs,
        in_specs=[SMEM] * smem + [VM] * (len(ins) - smem),
        out_specs=jax.tree.map(lambda _: VM, outs),
        scratch_shapes=list(scratch),
        compiler_params=pltpu.CompilerParams(vmem_limit_bytes=56 << 20),
        cost_estimate=pl.CostEstimate(flops=flops, transcendentals=0, bytes_accessed=4 << 20),
        name=name,
    )(*ins)


def S(shape, dtype):
    return jax.ShapeDtypeStruct(shape, dtype)


def prep_kernel(ids, q, k, v, g, kv_out, qg_out, sums_out):
    y = ids[1]
    order = order_matrix(False)
    squares = []
    for ref in (q, k):
        x = ref[...].astype(F32)
        squares.append(jnp.sum(x * x, axis=1, keepdims=True))
    lanes = lax.broadcasted_iota(jnp.int32, (SEG, DH), 1)
    both = jnp.where(lanes == 0, squares[0], 0.0) + jnp.where(lanes == 1, squares[1], 0.0)
    hi = both.astype(BF16)
    rest = both - hi.astype(F32)
    mid = rest.astype(BF16)
    low = (rest - mid.astype(F32)).astype(BF16)
    moved = nn(order, hi) + nn(order, mid) + nn(order, low)
    sums_out[...] = jnp.transpose(moved)[0:8]
    for out, index, ref in ((kv_out, 0, k), (kv_out, 1, v), (qg_out, 0, q), (qg_out, 1, g)):
        for s in range(4):
            part = ref[:, slab((y + s) % 4)]
            out[s, index] = nn(order, part).astype(BF16)


def inverse_rows(stats, which):
    rows = []
    for c in range(4):
        total = stats[8 * c, which : which + 1]
        for h in range(1, 8):
            total = total + stats[8 * c + h, which : which + 1]
        rows.append(lax.rsqrt(total / D + EPSILON))
    return rows


def normed(raw, inverse, gain):
    t = jnp.transpose(raw.astype(F32)) * inverse * gain
    return jnp.transpose(t).astype(BF16)


def place_v_kernel(ids, p0, p1, p2, p3, out):
    y = ids[1]
    for s, piece in enumerate((p0, p1, p2, p3)):
        out[(y + 4 - s) % 4] = piece[1].reshape(4, 128, DH)


def norm_k_kernel(ids, p0, p1, p2, p3, stats, gain, out):
    y = ids[1]
    inv = jnp.concatenate(inverse_rows(stats, 1), axis=0)
    keep = lax.broadcasted_iota(jnp.int32, (4, SEG), 0)
    for s, piece in enumerate((p0, p1, p2, p3)):
        c = (y + 4 - s) % 4
        row = jnp.sum(jnp.where(keep == c, inv, 0.0), axis=0, keepdims=True)
        out[c] = normed(piece[0], row, gain[...]).reshape(4, 128, DH)


def norm_q_kernel(ids, p0, p1, p2, p3, stats, gain, q_out, g_out):
    y = ids[1]
    inv = jnp.concatenate(inverse_rows(stats, 0), axis=0)
    keep = lax.broadcasted_iota(jnp.int32, (4, SEG), 0)
    for s, piece in enumerate((p0, p1, p2, p3)):
        c = (y + 4 - s) % 4
        row = jnp.sum(jnp.where(keep == c, inv, 0.0), axis=0, keepdims=True)
        q_out[c] = normed(piece[0], row, gain[...]).reshape(4, 128, DH)
        g_out[c] = piece[1].reshape(4, 128, DH)


def head_bits(ids):
    h = 4 * ids[2] + ids[1]
    par = h & 1
    return par, 2 * par + ((h >> 1) & 1), (h >> 2) & 1


def forward_part(keys, vals, q, score_ref, mask=None):
    count = len(keys)
    top = None
    for j in range(count):
        s = nt(keys[j](), q) * SCALE
        score_ref[j] = s
        t = jnp.max(s, axis=0, keepdims=True)
        top = t if top is None else jnp.maximum(top, t)
    if mask is not None:
        top = jnp.where(mask, top, FLOOR)
    total, summed = None, None
    for j in range(count):
        w = jnp.exp(score_ref[j] - top)
        if mask is not None:
            w = jnp.where(mask, w, 0.0)
        score_ref[j] = w
        t = jnp.sum(w, axis=0, keepdims=True)
        a = tn(vals[j](), w.astype(BF16))
        total = t if total is None else total + t
        summed = a if summed is None else summed + a
    return top, total, summed


def merge(m_ref, l_ref, a_ref, at, top, total, summed):
    m = m_ref[at]
    new = jnp.maximum(m, top)
    old_f = jnp.exp(m - new)
    new_f = jnp.exp(top - new)
    m_ref[at] = new
    l_ref[at] = old_f * l_ref[at] + new_f * total
    a_ref[at] = old_f * a_ref[at] + new_f * summed


def cut(x, b):
    return x[:, b * 128 : (b + 1) * 128]


def level_forward_kernel(ids, q, k, v, m_out, l_out, a_out, score):
    par, quarter, _ = head_bits(ids)

    def level0(c, carry):
        top, total, summed = forward_part(
            [lambda j=j: k[c, j] for j in range(4)],
            [lambda j=j: v[c, j] for j in range(4)],
            q[c].reshape(SEG, DH),
            score,
        )
        for b in range(4):
            m_out[c, b] = cut(top, b)
            l_out[c, b] = cut(total, b)
            a_out[c, b] = cut(summed, b)
        return carry

    lax.fori_loop(0, 4, level0, 0)

    def level1(s, carry):
        spots = [(2 * s + i // 2, 2 * par + i % 2) for i in range(4)]
        rows = jnp.concatenate([q[c, b] for c, b in spots], axis=0)
        top, total, summed = forward_part(
            [lambda c=c, b=b: k[c, b] for c, b in spots],
            [lambda c=c, b=b: v[c, b] for c, b in spots],
            rows,
            score,
        )
        for i, at in enumerate(spots):
            merge(m_out, l_out, a_out, at, cut(top, i), cut(total, i), cut(summed, i))
        return carry

    lax.fori_loop(0, 2, level1, 0)
    spots = [(i, quarter) for i in range(4)]
    rows = jnp.concatenate([q[c, b] for c, b in spots], axis=0)
    top, total, summed = forward_part(
        [lambda c=c, b=b: k[c, b] for c, b in spots],
        [lambda c=c, b=b: v[c, b] for c, b in spots],
        rows,
        score,
    )
    for i, at in enumerate(spots):
        merge(m_out, l_out, a_out, at, cut(top, i), cut(total, i), cut(summed, i))


def backward_chunk(w, factor, key, val, q, g, delta):
    soft = w if factor is None else w * factor
    grad_soft = nt(val, g)
    grad = (soft * (grad_soft - delta)).astype(BF16)
    grad_q = tn(key, grad)
    grad_k = nn(grad, q) * SCALE
    grad_v = nn(soft.astype(BF16), g)
    return grad_q, grad_k, grad_v


def main_kernel(
    ids, lists, q, g, k0, v0, k1, v1, k2, v2, k3, v3, m_in, l_in, a_in,
    att_out, dq_out, lse_out, delta_out, send1, send2, send3, dk_own, dv_own,
    kall, vall, dk, dv, score, score3, m, l, a,
):
    z, y = ids[0], ids[1]
    par, quarter, half = head_bits(ids)
    for i, (kk, vv) in enumerate(((k0, v0), (k1, v1), (k2, v2), (k3, v3))):
        kall[i] = kk[...]
        vall[i] = vv[...]
        dk[i] = jnp.zeros((4, 4, 128, DH), F32)
        dv[i] = jnp.zeros((4, 4, 128, DH), F32)
    m[...] = m_in[...]
    l[...] = l_in[...]
    a[...] = a_in[...]

    partner = jnp.where(z % 2 == 0, 1, 3)
    halves = pl.ds(pl.multiple_of(half * 64, 64), 64)
    rels = (0, 0, partner, partner)
    mask = (lax.broadcasted_iota(jnp.int32, (1, SEG), 1) % 128) // 64 == half

    def pair(ref, j):
        c = 2 * (j % 2)
        return jnp.concatenate([ref[rels[j], c, quarter, halves], ref[rels[j], c + 1, quarter, halves]], axis=0)

    q3 = jnp.concatenate([q[c, quarter] for c in range(4)], axis=0)
    g3 = jnp.concatenate([g[c, quarter] for c in range(4)], axis=0)
    top3, total, summed = forward_part(
        [lambda j=j: pair(kall, j) for j in range(4)],
        [lambda j=j: pair(vall, j) for j in range(4)],
        q3,
        score3,
        mask,
    )
    for i in range(4):
        merge(m, l, a, (i, quarter), cut(top3, i), cut(total, i), cut(summed, i))

    def place(c, j):
        block = lists[4 * z + c, j]
        owner = block // 4
        return ((owner // 4) + 4 - z) % 4, owner % 4, block % 4

    def runs(lb):
        return [
            (rb // 2, pl.ds(pl.multiple_of((rb % 2) * 64 + lb * 16, 16), 16)) for rb in range(8)
        ]

    def load(ref, c, j):
        rel, cc, lb = place(c, j)
        return jnp.concatenate([ref[rel, cc, b, r] for b, r in runs(lb)], axis=0)

    def add(ref, c, j, term):
        rel, cc, lb = place(c, j)
        for i, (b, r) in enumerate(runs(lb)):
            ref[rel, cc, b, r] = ref[rel, cc, b, r] + term[16 * i : 16 * (i + 1)]

    def one_ctx(c, carry):
        rows = q[c].reshape(SEG, DH)
        grows = g[c].reshape(SEG, DH)
        top, total, summed = forward_part(
            [lambda j=j: load(kall, c, j) for j in range(8)],
            [lambda j=j: load(vall, c, j) for j in range(8)],
            rows,
            score,
        )
        for b in range(4):
            merge(m, l, a, (c, b), cut(top, b), cut(total, b), cut(summed, b))
        joint = jnp.concatenate([m[c, b] for b in range(4)], axis=1)
        whole = jnp.concatenate([l[c, b] for b in range(4)], axis=1)
        merged = jnp.concatenate([a[c, b] for b in range(4)], axis=1) / whole
        lse = joint + jnp.log(whole)
        delta = jnp.sum(jnp.transpose(grows.astype(F32)) * merged, axis=0, keepdims=True)
        att_out[(c + 4 - y) % 4] = jnp.transpose(merged).astype(BF16)
        lse_out[c] = lse
        delta_out[c] = delta
        factor = jnp.exp(top - lse)
        grad_q = None
        for j in range(8):
            gq, gk, gv = backward_chunk(
                score[j], factor, load(kall, c, j), load(vall, c, j), rows, grows, delta
            )
            grad_q = gq if grad_q is None else grad_q + gq
            add(dk, c, j, gk.astype(BF16).astype(F32))
            add(dv, c, j, gv.astype(BF16).astype(F32))
        grad_q = grad_q * SCALE
        for b in range(4):
            dq_out[c, b] = cut(grad_q, b)
        return carry

    lax.fori_loop(0, 4, one_ctx, 0)

    def take(ref):
        row = [cut(ref[c], b) for c in range(4) for b in range(4)]
        return row

    def pick(ref):
        parts = []
        for c in range(4):
            out = cut(ref[c], 0)
            for b in range(1, 4):
                out = jnp.where(quarter == b, cut(ref[c], b), out)
            parts.append(out)
        return jnp.concatenate(parts, axis=1)

    lse3, delta3 = pick(lse_out), pick(delta_out)
    factor3 = jnp.exp(top3 - lse3)
    grad_q = None
    for j in range(4):
        gq, gk, gv = backward_chunk(score3[j], factor3, pair(kall, j), pair(vall, j), q3, g3, delta3)
        grad_q = gq if grad_q is None else grad_q + gq
        c = 2 * (j % 2)
        for i in range(2):
            at = (rels[j], c + i, quarter, halves)
            dk[at] = dk[at] + gk[64 * i : 64 * (i + 1)]
            dv[at] = dv[at] + gv[64 * i : 64 * (i + 1)]
    for i in range(4):
        dq_out[i, quarter] = dq_out[i, quarter] + cut(grad_q, i) * SCALE
    for rel, out in ((1, send1), (2, send2), (3, send3)):
        out[0] = dk[rel].astype(BF16)
        out[1] = dv[rel].astype(BF16)
    dk_own[...] = dk[0]
    dv_own[...] = dv[0]


def level_backward_kernel(
    ids, q, g, k, v, lse, delta, dq_in, dk_in, dv_in, p0, p1, p2, p3, gain, dk, dv, adj_out, raw_out, s_out, dq,
):
    y = ids[1]
    par, quarter, _ = head_bits(ids)
    dq[...] = dq_in[...]
    dk[...] = dk_in[...]
    dv[...] = dv_in[...]

    def row(ref, c, b):
        out = cut(ref[c], 0)
        for i in range(1, 4):
            out = jnp.where(b == i, cut(ref[c], i), out)
        return out

    def part(spots, rows, grows, logs, deltas):
        grad_q = None
        for c, b in spots:
            s = nt(k[c, b], rows) * SCALE
            soft = jnp.exp(s - logs)
            gq, gk, gv = backward_chunk(soft, None, k[c, b], v[c, b], rows, grows, deltas)
            grad_q = gq if grad_q is None else grad_q + gq
            dk[c, b] = dk[c, b] + gk
            dv[c, b] = dv[c, b] + gv
        grad_q = grad_q * SCALE
        for i, (c, b) in enumerate(spots):
            dq[c, b] = dq[c, b] + cut(grad_q, i)

    def gather(spots):
        return (
            jnp.concatenate([q[c, b] for c, b in spots], axis=0),
            jnp.concatenate([g[c, b] for c, b in spots], axis=0),
            jnp.concatenate([row(lse, c, b) for c, b in spots], axis=1),
            jnp.concatenate([row(delta, c, b) for c, b in spots], axis=1),
        )

    def level0(c, carry):
        part([(c, b) for b in range(4)], q[c].reshape(SEG, DH), g[c].reshape(SEG, DH), lse[c], delta[c])
        return carry

    lax.fori_loop(0, 4, level0, 0)

    def level1(s, carry):
        spots = [(2 * s + i // 2, 2 * par + i % 2) for i in range(4)]
        part(spots, *gather(spots))
        return carry

    lax.fori_loop(0, 2, level1, 0)
    spots = [(i, quarter) for i in range(4)]
    part(spots, *gather(spots))
    for s, piece in enumerate((p0, p1, p2, p3)):
        c = (y + 4 - s) % 4
        raw = jnp.transpose(piece[0].astype(F32))
        adj = jnp.concatenate([dq[c, b] for b in range(4)], axis=1) * gain[...]
        adj_out[c] = adj
        raw_out[c] = raw
        s_out[c] = jnp.sum(raw * adj, axis=0, keepdims=True)


def final_rows(inner, stats, which, adj, raw, y, out):
    inv = jnp.concatenate(inverse_rows(stats, which), axis=0)
    for c in range(4):
        total = inner[0, c : c + 1]
        for i in range(1, 32):
            total = total + inner[i, c : c + 1]
        r = inv[c : c + 1]
        grads = r * adj[c] - raw[c] * (r * r * r) * total / D
        out[(c + 4 - y) % 4] = jnp.transpose(grads).astype(BF16)


def final_q_kernel(ids, inner, stats, adj, raw, out):
    final_rows(inner, stats, 0, adj, raw, ids[1], out)


def collect_kernel(ids, dk, dv, r1, r2, r3, p0, p1, p2, p3, gain, dv_out, adj_out, raw_out, s_out):
    y = ids[1]
    for s, piece in enumerate((p0, p1, p2, p3)):
        c = (y + 4 - s) % 4
        sums = []
        for i, own in enumerate((dk, dv)):
            total = own[c]
            for r in (r1, r2, r3):
                total = total + r[i, c].astype(F32)
            sums.append(total.reshape(SEG, DH))
        dv_out[(c + 4 - y) % 4] = sums[1].astype(BF16)
        raw = jnp.transpose(piece[0].astype(F32))
        adj = jnp.transpose(sums[0]) * gain[...]
        adj_out[c] = adj
        raw_out[c] = raw
        s_out[c] = jnp.sum(raw * adj, axis=0, keepdims=True)


def final_k_kernel(ids, inner, stats, adj, raw, out):
    final_rows(inner, stats, 1, adj, raw, ids[1], out)


def restore_kernel(ids, *refs):
    y = ids[1]
    order = order_matrix(True)
    count = len(refs) // 5
    outs = refs[4 * count :]
    for n in range(count):
        for s in range(4):
            piece = refs[4 * n + s][...]
            outs[n][:, slab((y + 4 - s) % 4)] = nn(order, piece).astype(BF16)


def shift(value, axis, step):
    return lax.ppermute(value, axis, [(i, (i + step) % 4) for i in range(4)])


def y_exchange(slots):
    return [slots[0], shift(slots[1], "y", 1), shift(slots[2], "y", 2), shift(slots[3], "y", -1)]


def y_return(slots):
    return y_exchange(slots)


def to_all(value):
    copies = jnp.broadcast_to(value, (32, *value.shape))
    return lax.all_to_all(copies, ("y", "head"), split_axis=0, concat_axis=0, tiled=True)


def shards(queries, key_states, values, query_gain, key_gain, memory_blocks, cotangent):
    z, y, hd = lax.axis_index("z"), lax.axis_index("y"), lax.axis_index("head")
    ids = jnp.stack([z, y, hd]).astype(jnp.int32)

    def gain_of(gain):
        own = lax.dynamic_index_in_dim(gain.reshape(4, DH), y, 0, keepdims=False)
        return own.astype(F32)[:, None]

    q_gain, k_gain = gain_of(query_gain), gain_of(key_gain)
    head4 = (4, 4, 128, DH)
    kv, qg, sums = call(
        prep_kernel,
        (ids, queries, key_states, values, cotangent),
        1,
        (S((4, 2, SEG, DH), BF16), S((4, 2, SEG, DH), BF16), S((8, SEG), F32)),
        flops=4 * 2 * SEG**3,
        name="prep",
    )
    kv_pieces = y_exchange(kv)
    stats = to_all(sums[:2])
    qg_pieces = y_exchange(qg)
    v0 = call(place_v_kernel, (ids, *kv_pieces), 1, S(head4, BF16), name="place_v")
    v3, v1 = shift(v0, "z", 1), shift(v0, "z", -1)
    k0 = call(norm_k_kernel, (ids, *kv_pieces, stats, k_gain), 1, S(head4, BF16), name="norm_k")
    k3, k1 = shift(k0, "z", 1), shift(k0, "z", -1)
    v2, k2 = shift(v1, "z", -1), shift(k3, "z", 1)
    q, g = call(
        norm_q_kernel,
        (ids, *qg_pieces, stats, q_gain),
        1,
        (S(head4, BF16), S(head4, BF16)),
        name="norm_q",
    )
    row4 = S((4, 4, 1, 128), F32)
    m, l, a = call(
        level_forward_kernel,
        (ids, q, k0, v0),
        1,
        (row4, row4, S(head4, F32)),
        [pltpu.VMEM((4, 128, SEG), F32)],
        flops=7 * 2 * 2 * 512 * 512 * 128,
        name="level_forward",
    )
    row = S((4, 1, SEG), F32)
    send = S((2, *head4), BF16)
    att, dq, lse, delta, send1, send2, send3, dk, dv = call(
        main_kernel,
        (ids, memory_blocks, q, g, k0, v0, k1, v1, k2, v2, k3, v3, m, l, a),
        2,
        (S((4, SEG, DH), BF16), S(head4, F32), row, row, send, send, send, S(head4, F32), S(head4, F32)),
        [
            pltpu.VMEM((4, *head4), BF16),
            pltpu.VMEM((4, *head4), BF16),
            pltpu.VMEM((4, *head4), F32),
            pltpu.VMEM((4, *head4), F32),
            pltpu.VMEM((8, 128, SEG), F32),
            pltpu.VMEM((4, 128, SEG), F32),
            pltpu.VMEM((4, 4, 1, 128), F32),
            pltpu.VMEM((4, 4, 1, 128), F32),
            pltpu.VMEM(head4, F32),
        ],
        flops=4 * 6 * 2 * 512 * 1024 * 128,
        name="main",
    )
    back2, back1, back3 = shift(send2, "z", 2), shift(send1, "z", 1), shift(send3, "z", -1)
    att_pieces = y_return(att)
    wide = S((4, DH, SEG), F32)
    dk, dv, q_adj, q_raw, q_s = call(
        level_backward_kernel,
        (ids, q, g, k0, v0, lse, delta, dq, dk, dv, *qg_pieces, q_gain),
        1,
        (S(head4, F32), S(head4, F32), wide, wide, row),
        [pltpu.VMEM(head4, F32)],
        flops=7 * 5 * 2 * 512 * 512 * 128,
        name="level_backward",
    )
    q_inner = to_all(q_s.reshape(4, SEG))
    dq_slots = call(
        final_q_kernel, (ids, q_inner, stats, q_adj, q_raw), 1, S((4, SEG, DH), BF16), name="final_q"
    )
    dq_pieces = y_return(dq_slots)
    dv_slots, k_adj, k_raw, k_s = call(
        collect_kernel,
        (ids, dk, dv, back1, back2, back3, *kv_pieces, k_gain),
        1,
        (S((4, SEG, DH), BF16), wide, wide, row),
        name="collect",
    )
    k_inner = to_all(k_s.reshape(4, SEG))
    dv_pieces = y_return(dv_slots)
    dk_slots = call(
        final_k_kernel, (ids, k_inner, stats, k_adj, k_raw), 1, S((4, SEG, DH), BF16), name="final_k"
    )
    dk_pieces = y_return(dk_slots)
    flat = S((SEG, 4 * DH), BF16)
    attended, query_grads, value_grads = call(
        restore_kernel,
        (ids, *att_pieces, *dq_pieces, *dv_pieces),
        1,
        (flat, flat, flat),
        name="restore",
    )
    (key_grads,) = call(restore_kernel, (ids, *dk_pieces), 1, (flat,), name="restore_k")
    return (attended, query_grads, key_grads, value_grads)


def solution(mesh):
    split = Mesh(mesh.devices.reshape(4, 4, 8), ("z", "y", "head"))
    big = P(("z", "y"), "head")
    in_specs = (big, big, big, P("head"), P("head"), P(), big)
    return jax.shard_map(
        shards, mesh=split, in_specs=in_specs, out_specs=(big, big, big, big), check_vma=False
    )
```

```python
import math

import jax
import jax.numpy as jnp
from jax import lax
from jax.experimental import pallas as pl
from jax.experimental.pallas import tpu as pltpu
from jax.sharding import Mesh
from jax.sharding import PartitionSpec as P

DH = 128
D = 4096
SEG = 512
EPSILON = 1e-06
FLOOR = -1e30
SCALE = 1.0 / math.sqrt(DH)
F32 = jnp.float32
BF16 = jnp.bfloat16


def nt(a, b):
    return lax.dot_general(a, b, (((1,), (1,)), ((), ())), preferred_element_type=F32)


def nn(a, b):
    return lax.dot_general(a, b, (((1,), (0,)), ((), ())), preferred_element_type=F32)


def tn(a, b):
    return lax.dot_general(a, b, (((0,), (0,)), ((), ())), preferred_element_type=F32)


def order_matrix(transposed):
    row = lax.broadcasted_iota(jnp.int32, (SEG, SEG), 1 if transposed else 0)
    col = lax.broadcasted_iota(jnp.int32, (SEG, SEG), 0 if transposed else 1)
    rb = row >> 6
    residue = ((rb & 1) << 2) | (rb & 2) | (rb >> 2)
    return (col == ((row & 63) * 8 + residue)).astype(F32).astype(BF16)


def slab(index):
    return pl.ds(pl.multiple_of(index * DH, DH), DH)


SMEM = pl.BlockSpec(memory_space=pltpu.SMEM)
VM = pl.BlockSpec(memory_space=pltpu.VMEM)


def call(body, ins, smem, outs, scratch=(), flops=0, far=(), rows=None, room=24):
    return call_inner(body, ins, smem, outs, scratch, flops, far, rows, room)


def call_inner(body, ins, smem, outs, scratch, flops, far, rows, room):
    specs = [SMEM] * smem + [VM] * (len(ins) - smem)
    for i in far:
        specs[i] = pl.BlockSpec(memory_space=pl.ANY)
    for i, at in (rows or {}).items():
        shape = (1, *ins[i].shape[1:])
        specs[i] = pl.BlockSpec(shape, lambda *_, at=at: (at, 0, 0, 0, 0))
    return pl.pallas_call(
        body,
        out_shape=outs,
        grid=(1,) if rows else (),
        in_specs=specs,
        out_specs=jax.tree.map(lambda _: VM, outs),
        scratch_shapes=list(scratch),
        compiler_params=pltpu.CompilerParams(vmem_limit_bytes=room << 20),
        cost_estimate=pl.CostEstimate(flops=flops, transcendentals=0, bytes_accessed=4 << 20),
    )(*ins)


def S(shape, dtype):
    return jax.ShapeDtypeStruct(shape, dtype)


def ordered_slots(y, order, ref, outs):
    ones = jnp.ones((8, DH), BF16)
    squares = jnp.zeros((8, SEG), F32)
    for s in range(4):
        x = nn(order, ref[:, slab((y + s) % 4)])
        outs[s][...] = x.astype(BF16)
        square = x * x
        high = square.astype(BF16)
        low = (square - high.astype(F32)).astype(BF16)
        squares = squares + nt(ones, high) + nt(ones, low)
    return squares


def prep_v_kernel(ids, v, o0, o1, o2, o3):
    order = order_matrix(False)
    for s, out in enumerate((o0, o1, o2, o3)):
        out[...] = nn(order, v[:, slab((ids[1] + s) % 4)]).astype(BF16)


def prep_k_kernel(ids, k, o0, o1, o2, o3, sums_out):
    sums_out[...] = ordered_slots(ids[1], order_matrix(False), k, (o0, o1, o2, o3))


def prep_qg_kernel(ids, q, g, key_sums, o0, o1, o2, o3, stats_out):
    y = ids[1]
    order = order_matrix(False)
    outs = (o0, o1, o2, o3)
    sums = ordered_slots(y, order, q, [out.at[0] for out in outs])
    both = jnp.concatenate([sums[0:1], key_sums[0:1]], axis=0)
    for i in range(32):
        stats_out[i] = both
    for s in range(4):
        outs[s][1] = nn(order, g[:, slab((y + s) % 4)]).astype(BF16)


def total_rows(ref, first, count, which):
    total = ref[first, which : which + 1]
    for i in range(1, count):
        total = total + ref[first + i, which : which + 1]
    return total


def inverse_row(stats, c, which):
    return lax.rsqrt(total_rows(stats, 8 * c, 8, which) / D + EPSILON)


def normed(raw, inverse, gain):
    t = jnp.transpose(raw.astype(F32)) * inverse * gain
    return jnp.transpose(t).astype(BF16)


def place_v_kernel(ids, p0, p1, p2, p3, out):
    y = ids[1]
    for s, piece in enumerate((p0, p1, p2, p3)):
        out[(y + 4 - s) % 4] = piece[...].reshape(4, 128, DH)


def gain_column(ids, gain):
    row = gain[:, slab(ids[1])].astype(F32)
    return jnp.transpose(jnp.broadcast_to(row, (DH, DH)))[:, 0:1]


def norm_k_kernel(ids, p0, p1, p2, p3, stats, gain, out):
    y = ids[1]
    scale = gain_column(ids, gain)
    for s, piece in enumerate((p0, p1, p2, p3)):
        c = (y + 4 - s) % 4
        out[c] = normed(piece[...], inverse_row(stats, c, 1), scale).reshape(4, 128, DH)


def head_bits(ids):
    h = 4 * ids[2] + ids[1]
    par = h & 1
    return par, 2 * par + ((h >> 1) & 1), (h >> 2) & 1


def forward_part(keys, vals, q, score_ref, mask=None, keep=False):
    count = len(keys)
    top = None
    for j in range(count):
        s = nt(keys[j](), q) * SCALE
        score_ref[j] = s
        t = jnp.max(s, axis=0, keepdims=True)
        top = t if top is None else jnp.maximum(top, t)
    if mask is not None:
        top = jnp.where(mask, top, FLOOR)
    total, summed = None, None
    for j in range(count):
        w = jnp.exp(score_ref[j] - top)
        if mask is not None:
            w = jnp.where(mask, w, 0.0)
        if keep:
            score_ref[j] = w
        t = jnp.sum(w, axis=0, keepdims=True)
        a = tn(vals[j](), w.astype(BF16))
        total = t if total is None else total + t
        summed = a if summed is None else summed + a
    return top, total, summed


def merge(m_ref, l_ref, a_ref, at, top, total, summed):
    m = m_ref[at]
    new = jnp.maximum(m, top)
    old_f = jnp.exp(m - new)
    new_f = jnp.exp(top - new)
    m_ref[at] = new
    l_ref[at] = old_f * l_ref[at] + new_f * total
    a_ref[at] = old_f * a_ref[at] + new_f * summed


def cut(x, b):
    return x[:, b * 128 : (b + 1) * 128]


def rows_of(ref, spots):
    return jnp.concatenate([ref[c, b] for c, b in spots], axis=0)


def chunks_of(ref, spots):
    return [lambda at=spots[i : i + PER]: rows_of(ref, at) for i in range(0, len(spots), PER)]


def level_forward_kernel(ids, p0, p1, p2, p3, stats, gain, k, v, q, g, m_out, l_out, a_out, score):
    y = ids[1]
    par, quarter, _ = head_bits(ids)
    scale = gain_column(ids, gain)
    for s, piece in enumerate((p0, p1, p2, p3)):
        c = (y + 4 - s) % 4
        q[c] = normed(piece[0], inverse_row(stats, c, 0), scale).reshape(4, 128, DH)
        g[c] = piece[1].reshape(4, 128, DH)

    def level0(c, carry):
        spots = [(c, b) for b in range(4)]
        top, total, summed = forward_part(
            chunks_of(k, spots), chunks_of(v, spots), rows_of(q, spots), score
        )
        for b in range(4):
            m_out[c, b] = cut(top, b)
            l_out[c, b] = cut(total, b)
            a_out[c, b] = cut(summed, b)
        return carry

    lax.fori_loop(0, 4, level0, 0)

    def joined(spots):
        top, total, summed = forward_part(
            chunks_of(k, spots), chunks_of(v, spots), rows_of(q, spots), score
        )
        for i, at in enumerate(spots):
            merge(m_out, l_out, a_out, at, cut(top, i), cut(total, i), cut(summed, i))

    def level1(s, carry):
        joined([(2 * s + i // 2, 2 * par + i % 2) for i in range(4)])
        return carry

    lax.fori_loop(0, 2, level1, 0)
    joined([(i, quarter) for i in range(4)])


def backward_chunk(key, val, q, g, lse, delta, mask=None):
    soft = jnp.exp(nt(key, q) * SCALE - lse)
    if mask is not None:
        soft = jnp.where(mask, soft, 0.0)
    grad = (soft * (nt(val, g) - delta)).astype(BF16)
    return tn(key, grad), nn(grad, q) * SCALE, nn(soft.astype(BF16), g)


def place(ids, lists, c, j):
    block = lists[j, 4 * ids[0] + c]
    owner = block // 4
    return ((owner // 4) + 4 - ids[0]) % 4, owner % 4, block % 4


def runs(lb):
    return [(rb // 2, pl.ds(pl.multiple_of((rb % 2) * 64 + lb * 16, 16), 16)) for rb in range(8)]


def level3_spots(ids):
    _, quarter, half = head_bits(ids)
    halves = pl.ds(pl.multiple_of(half * 64, 64), 64)
    mask = (lax.broadcasted_iota(jnp.int32, (1, SEG), 1) % 128) // 64 == half
    partner = jnp.where(ids[0] % 2 == 0, 1, 3)
    return quarter, halves, mask, partner


def quarter_row(ref, c, quarter):
    out = cut(ref[c], 0)
    for i in range(1, 4):
        out = jnp.where(quarter == i, cut(ref[c], i), out)
    return out


def kept_part(w, factor, key, val, q, g, delta):
    soft = w * factor
    grad = (soft * (nt(val, g) - delta)).astype(BF16)
    return tn(key, grad), nn(grad, q) * SCALE, nn(soft.astype(BF16), g)


def main_kernel(
    ids, lists, q, g, k0, v0, k1, v1, k2, v2, k3, v3, m_in, l_in, a_in,
    att, dq, lse_out, delta_out, dk_own, dv_own, v_up, v_down, k_up, k_down, vp, vn, kp, kn,
    kall, vall, dk, dv, score, score3, m, l, a, sems,
):
    quarter, halves, mask, partner = level3_spots(ids)
    copies = [
        pltpu.make_async_copy(src, dst.at[i], sems.at[n, i])
        for n, (dst, group) in enumerate(((kall, (k0, k1, k2, k3)), (vall, (v0, v1, v2, v3))))
        for i, src in enumerate(group)
    ]
    for copy in copies:
        copy.start()
    m[...] = m_in[...]
    l[...] = l_in[...]
    a[...] = a_in[...]
    dk[...] = jnp.zeros(dk.shape, F32)
    dv[...] = jnp.zeros(dv.shape, F32)
    for copy in copies:
        copy.wait()

    spots3 = [(at, c, quarter, halves) for at in (0, partner) for c in range(4)]
    rows3 = [(c, quarter) for c in range(4)]

    def eight(ref):
        return jnp.concatenate([ref[at] for at in spots3], axis=0)

    top3, total, summed = forward_part(
        [lambda: eight(kall)], [lambda: eight(vall)], rows_of(q, rows3), score3, mask, True
    )
    for i in range(4):
        merge(m, l, a, (i, quarter), cut(top3, i), cut(total, i), cut(summed, i))

    def one_ctx(c, carry):
        rows = q[c].reshape(SEG, DH)
        grows = g[c].reshape(SEG, DH)
        groups = []
        for i in (0, 4):
            spots = []
            for j in range(i, i + 4):
                rel, cc, lb = place(ids, lists, c, j)
                spots += [(rel, cc, b, r) for b, r in runs(lb)]
            groups.append(spots)

        def blocks(ref):
            return [lambda at=at: jnp.concatenate([ref[x] for x in at], axis=0) for at in groups]

        keys, vals = blocks(kall), blocks(vall)
        top, total, summed = forward_part(keys, vals, rows, score, None, True)
        for b in range(4):
            merge(m, l, a, (c, b), cut(top, b), cut(total, b), cut(summed, b))
        joint = jnp.concatenate([m[c, b] for b in range(4)], axis=1)
        whole = jnp.concatenate([l[c, b] for b in range(4)], axis=1)
        merged = jnp.concatenate([a[c, b] for b in range(4)], axis=1) / whole
        att[c] = merged.astype(BF16)
        lse = joint + jnp.log(whole)
        delta = jnp.sum(jnp.transpose(grows.astype(F32)) * merged, axis=0, keepdims=True)
        lse_out[c] = lse
        delta_out[c] = delta
        factor = jnp.exp(top - lse)
        grad_q = None
        for n, spots in enumerate(groups):
            gq, gk, gv = kept_part(score[n], factor, keys[n](), vals[n](), rows, grows, delta)
            grad_q = gq if grad_q is None else grad_q + gq
            gk = gk.astype(BF16).astype(F32)
            gv = gv.astype(BF16).astype(F32)
            for i, spot in enumerate(spots):
                dk[spot] = dk[spot] + gk[16 * i : 16 * (i + 1)]
                dv[spot] = dv[spot] + gv[16 * i : 16 * (i + 1)]
        for b in range(4):
            dq[c, b] = cut(grad_q, b) * SCALE
        return carry

    lax.fori_loop(0, 4, one_ctx, 0)
    logs = jnp.concatenate([quarter_row(lse_out, c, quarter) for c in range(4)], axis=1)
    deltas = jnp.concatenate([quarter_row(delta_out, c, quarter) for c in range(4)], axis=1)
    gq, gk, gv = kept_part(
        score3[0], jnp.exp(top3 - logs), eight(kall), eight(vall), rows_of(q, rows3), rows_of(g, rows3), deltas
    )
    for c in range(4):
        dq[c, quarter] = dq[c, quarter] + cut(gq, c) * SCALE
    for n, spot in enumerate(spots3):
        dk[spot] = dk[spot] + gk[64 * n : 64 * (n + 1)]
        dv[spot] = dv[spot] + gv[64 * n : 64 * (n + 1)]
    dk_own[...] = dk[0]
    dv_own[...] = dv[0]
    for ref, up, down, up_kept, down_kept in ((dv, v_up, v_down, vp, vn), (dk, k_up, k_down, kp, kn)):
        up[0] = ref[2, 0:2].astype(BF16)
        up[1] = ref[1, 2:4].astype(BF16)
        down[0] = ref[2, 2:4].astype(BF16)
        down[1] = ref[3, 0:2].astype(BF16)
        up_kept[...] = ref[1, 0:2]
        down_kept[...] = ref[3, 2:4]


def relay_kernel(up, down, from_below, from_above, up_out, down_out):
    up_out[...] = (up[...] + from_below[0].astype(F32)).astype(BF16)
    down_out[...] = (down[...] + from_above[0].astype(F32)).astype(BF16)


def put_pair(out, x):
    high = x.astype(BF16)
    out[0] = high
    out[1] = (x - high.astype(F32)).astype(BF16)


def main3_kernel(
    ids, q, g, k, v, lse, delta, dq_in, dk_in, dv_in, p0, p1, p2, p3, gain, att,
    dk, dv, a0, a1, a2, a3, s_out, dq,
):
    y = ids[1]
    par, quarter, _ = head_bits(ids)
    dq[...] = dq_in[...]
    dk[...] = dk_in[...]
    dv[...] = dv_in[...]

    def part(spots, rows, grows, logs, deltas):
        for i in range(0, 4, PER):
            at = spots[i : i + PER]
            gq, gk, gv = backward_chunk(rows_of(k, at), rows_of(v, at), rows, grows, logs, deltas)
            for n, (c, b) in enumerate(at):
                dk[c, b] = dk[c, b] + gk[128 * n : 128 * (n + 1)]
                dv[c, b] = dv[c, b] + gv[128 * n : 128 * (n + 1)]
            for n, (c, b) in enumerate(spots):
                dq[c, b] = dq[c, b] + cut(gq, n) * SCALE

    def gather(spots):
        return (
            rows_of(q, spots),
            rows_of(g, spots),
            jnp.concatenate([quarter_row(lse, c, b) for c, b in spots], axis=1),
            jnp.concatenate([quarter_row(delta, c, b) for c, b in spots], axis=1),
        )

    def level0(c, carry):
        part([(c, b) for b in range(4)], q[c].reshape(SEG, DH), g[c].reshape(SEG, DH), lse[c], delta[c])
        return carry

    lax.fori_loop(0, 4, level0, 0)

    def level1(s, carry):
        spots = [(2 * s + i // 2, 2 * par + i % 2) for i in range(4)]
        part(spots, *gather(spots))
        return carry

    lax.fori_loop(0, 2, level1, 0)
    spots = [(i, quarter) for i in range(4)]
    part(spots, *gather(spots))
    pieces = (p0, p1, p2, p3)
    scale = gain_column(ids, gain)
    for s, out in enumerate((a0, a1, a2, a3)):
        c = (y + s) % 4
        raw = jnp.transpose(pieces[(4 - s) % 4][0].astype(F32))
        adj = jnp.concatenate([dq[c, b] for b in range(4)], axis=1) * scale
        put_pair(out, adj)
        out[2] = att[c]
        inner = jnp.sum(raw * adj, axis=0, keepdims=True)
        for h in range(8):
            s_out[8 * c + h] = inner


def add_rows(own, below1, above1, below2, above2, total):
    total[0:2] = own[0:2] + below2[...].astype(F32) + above1[0].astype(F32)
    total[2:4] = own[2:4] + below1[0].astype(F32) + above2[...].astype(F32)


def collect_v_kernel(ids, dv, below1, above1, below2, above2, o0, o1, o2, o3, total):
    add_rows(dv, below1, above1, below2, above2, total)
    for s, out in enumerate((o0, o1, o2, o3)):
        out[...] = jnp.transpose(total[(ids[1] + s) % 4].reshape(SEG, DH)).astype(BF16)


def collect_k_kernel(
    ids, dk, below1, above1, below2, above2, p0, p1, p2, p3, gain,
    o0, o1, o2, o3, s_out, total,
):
    add_rows(dk, below1, above1, below2, above2, total)
    pieces = (p0, p1, p2, p3)
    scale = gain_column(ids, gain)
    for s, out in enumerate((o0, o1, o2, o3)):
        c = (ids[1] + s) % 4
        raw = jnp.transpose(pieces[(4 - s) % 4][...].astype(F32))
        adj = jnp.transpose(total[c].reshape(SEG, DH)) * scale
        put_pair(out, adj)
        inner = jnp.sum(raw * adj, axis=0, keepdims=True)
        for h in range(8):
            s_out[8 * c + h] = inner


def restore_kernel(ids, p0, p1, p2, p3, out):
    y = ids[1]
    order = order_matrix(True)
    for s, piece in enumerate((p0, p1, p2, p3)):
        out[:, slab((y + 4 - s) % 4)] = nt(order, piece[...]).astype(BF16)


def finish_kernel(which, ids, inner, stats, raw, p0, p1, p2, p3, out, plain=None):
    y = ids[1]
    order = order_matrix(True)
    total = total_rows(inner, 0, 32, 0)
    r = inverse_row(stats, y, which)
    for s, piece in enumerate((p0, p1, p2, p3)):
        at = slab((y + 4 - s) % 4)
        x = tn(raw[:, at], order)
        adj = piece[0].astype(F32) + piece[1].astype(F32)
        grads = (r * adj - x * (r * r * r) * total / D).astype(BF16)
        out[:, at] = nt(order, grads).astype(BF16)
        if plain is not None:
            plain[:, at] = nt(order, piece[2]).astype(BF16)


def shift(value, axis, step):
    return lax.ppermute(value, axis, [(i, (i + step) % 4) for i in range(4)])


def y_exchange(slots):
    far = shift(slots[2], "y", 2)
    return [slots[0], shift(slots[1], "y", 1), far, shift(slots[3], "y", -1)]


def to_all(copies):
    return lax.all_to_all(copies, ("y", "head"), split_axis=0, concat_axis=0, tiled=True)


def shards_inner(queries, key_states, values, query_gain, key_gain, memory_blocks, cotangent):
    z, y, hd = lax.axis_index("z"), lax.axis_index("y"), lax.axis_index("head")
    ids = jnp.stack([z, y, hd]).astype(jnp.int32)

    q_gain, k_gain = query_gain.reshape(1, 4 * DH), key_gain.reshape(1, 4 * DH)
    lists = memory_blocks.T
    head4 = (4, 4, 128, DH)
    one, full = S(head4, BF16), S(head4, F32)
    slot = S((2, SEG, DH), BF16)
    back = S((3, DH, SEG), BF16)
    every = S((32, 1, SEG), F32)
    row, row4 = S((4, 1, SEG), F32), S((4, 4, 1, 128), F32)
    flat = S((SEG, 4 * DH), BF16)

    part = S((SEG, DH), BF16)
    v_slots = call(prep_v_kernel, (ids, values), 1, (part,) * 4)
    v_pieces = y_exchange(v_slots)
    *k_slots, sums = call(prep_k_kernel, (ids, key_states), 1, (part,) * 4 + (S((8, SEG), F32),))
    k_pieces = y_exchange(k_slots)
    *qg, sums = call(
        prep_qg_kernel, (ids, queries, cotangent, sums), 1, (slot,) * 4 + (S((32, 2, SEG), F32),)
    )
    stats = to_all(sums)
    qg_pieces = y_exchange(qg)
    v0 = call(place_v_kernel, (ids, *v_pieces), 1, one)
    v3, v1 = shift(v0, "z", 1), shift(v0, "z", -1)
    k0 = call(norm_k_kernel, (ids, *k_pieces, stats, k_gain), 1, one)
    k3, k1 = shift(k0, "z", 1), shift(k0, "z", -1)
    v2 = shift(v1, "z", -1)
    k2 = shift(k3, "z", 1)
    q, g, m, l, a = call(
        level_forward_kernel,
        (ids, *qg_pieces, stats, q_gain, k0, v0),
        1,
        (one, one, row4, row4, full),
        [pltpu.VMEM((4 // PER, 128 * PER, SEG), F32)],
        flops=7 * 2 * 2 * 512 * 512 * 128,
    )
    half, kept = S((2, 2, 4, 128, DH), BF16), S((2, 4, 128, DH), F32)
    att, dq, lse, delta, dk, dv, v_up, v_down, k_up, k_down, vp, vn, kp, kn = call(
        main_kernel,
        (ids, lists, q, g, k0, v0, k1, v1, k2, v2, k3, v3, m, l, a),
        2,
        (S((4, DH, SEG), BF16), full, row, row, full, full) + (half,) * 4 + (kept,) * 4,
        [
            pltpu.VMEM((4, *head4), BF16),
            pltpu.VMEM((4, *head4), BF16),
            pltpu.VMEM((4, *head4), F32),
            pltpu.VMEM((4, *head4), F32),
            pltpu.VMEM((2, SEG, SEG), F32),
            pltpu.VMEM((1, SEG, SEG), F32),
            pltpu.VMEM((4, 4, 1, 128), F32),
            pltpu.VMEM((4, 4, 1, 128), F32),
            pltpu.VMEM(head4, F32),
            pltpu.SemaphoreType.DMA((2, 4)),
        ],
        flops=9 * 6 * 2 * 512 * 512 * 128,
        far=range(4, 12),
        room=44,
    )
    v_below, v_above = shift(v_up, "z", 1), shift(v_down, "z", -1)
    k_below, k_above = shift(k_up, "z", 1), shift(k_down, "z", -1)
    dk, dv, *q_slots, q_s = call(
        main3_kernel,
        (ids, q, g, k0, v0, lse, delta, dq, dk, dv, *qg_pieces, q_gain, att),
        1,
        (full, full) + (back,) * 4 + (every,),
        [pltpu.VMEM(head4, F32)],
        flops=7 * 5 * 2 * 512 * 512 * 128,
    )

    def relayed(up, down, below, above):
        pair = S((2, 4, 128, DH), BF16)
        rows = {2: 0, 3: 0}
        return call(relay_kernel, (up, down, below, above), 0, (pair, pair), rows=rows)

    v_up, v_down = relayed(vp, vn, v_below, v_above)
    v_below2, v_above2 = shift(v_up, "z", 1), shift(v_down, "z", -1)
    k_up, k_down = relayed(kp, kn, k_below, k_above)
    k_below2, k_above2 = shift(k_up, "z", 1), shift(k_down, "z", -1)
    q_adj = y_exchange(q_slots)
    q_inner = to_all(q_s)
    v_slots = call(
        collect_v_kernel,
        (ids, dv, v_below, v_above, v_below2, v_above2),
        1,
        (S((DH, SEG), BF16),) * 4,
        [pltpu.VMEM(head4, F32)],
        rows={2: 1, 3: 1},
    )
    v_back = y_exchange(v_slots)
    query_grads, attended = call(
        lambda *refs: finish_kernel(0, *refs),
        (ids, q_inner, stats, queries, *q_adj),
        1,
        (flat, flat),
    )
    value_grads = call(restore_kernel, (ids, *v_back), 1, flat)
    *k_slots, k_s = call(
        collect_k_kernel,
        (ids, dk, k_below, k_above, k_below2, k_above2, *k_pieces, k_gain),
        1,
        (S((2, DH, SEG), BF16),) * 4 + (every,),
        [pltpu.VMEM(head4, F32)],
        rows={2: 1, 3: 1},
    )
    k_adj = y_exchange(k_slots)
    k_inner = to_all(k_s)
    key_grads = call(
        lambda *refs: finish_kernel(1, *refs), (ids, k_inner, stats, key_states, *k_adj), 1, flat
    )
    return (attended, query_grads, key_grads, value_grads)


PER = 4


def solution(mesh):
    split = Mesh(mesh.devices.reshape(4, 4, 8), ("z", "y", "head"))
    big = P(("z", "y"), "head")
    in_specs = (big, big, big, P("head"), P("head"), P(), big)
    return jax.shard_map(
        shards_inner, mesh=split, in_specs=in_specs, out_specs=(big, big, big, big), check_vma=False
    )
```

```python
import math

import jax
import jax.numpy as jnp
from jax import lax
from jax.experimental import pallas as pl
from jax.experimental.pallas import tpu as pltpu
from jax.sharding import Mesh
from jax.sharding import PartitionSpec as P

DH = 128
D = 4096
SEG = 512
EPSILON = 1e-06
FLOOR = -1e30
SCALE = 1.0 / math.sqrt(DH)
F32 = jnp.float32
BF16 = jnp.bfloat16


def nt(a, b):
    return lax.dot_general(a, b, (((1,), (1,)), ((), ())), preferred_element_type=F32)


def nn(a, b):
    return lax.dot_general(a, b, (((1,), (0,)), ((), ())), preferred_element_type=F32)


def tn(a, b):
    return lax.dot_general(a, b, (((0,), (0,)), ((), ())), preferred_element_type=F32)


def order_matrix(transposed):
    row = lax.broadcasted_iota(jnp.int32, (SEG, SEG), 1 if transposed else 0)
    col = lax.broadcasted_iota(jnp.int32, (SEG, SEG), 0 if transposed else 1)
    rb = row >> 6
    residue = ((rb & 1) << 2) | (rb & 2) | (rb >> 2)
    return (col == ((row & 63) * 8 + residue)).astype(F32).astype(BF16)


def slab(index):
    return pl.ds(pl.multiple_of(index * DH, DH), DH)


SMEM = pl.BlockSpec(memory_space=pltpu.SMEM)
VM = pl.BlockSpec(memory_space=pltpu.VMEM)


def call(body, ins, smem, outs, scratch=(), flops=0, far=(), room=18, fetch=()):
    return call_inner(body, ins, smem, outs, scratch, flops, far, room, fetch)


def call_inner(body, ins, smem, outs, scratch, flops, far, room, fetch):
    specs = [SMEM] * smem + [VM] * (len(ins) - smem)
    for i in far:
        specs[i] = pl.BlockSpec(memory_space=pl.ANY)
    body, scratch = fetching(body, ins, specs, scratch, fetch)
    return pl.pallas_call(
        body,
        out_shape=outs,
        in_specs=specs,
        out_specs=jax.tree.map(lambda _: VM, outs),
        scratch_shapes=list(scratch),
        compiler_params=pltpu.CompilerParams(vmem_limit_bytes=room << 20),
        cost_estimate=pl.CostEstimate(flops=flops, transcendentals=0, bytes_accessed=4 << 20),
    )(*ins)


def S(shape, dtype):
    return jax.ShapeDtypeStruct(shape, dtype)


def fetching(body, ins, specs, scratch, fetch):
    if not fetch:
        return body, scratch
    entry = fetch if isinstance(fetch, dict) else dict.fromkeys(fetch)
    extra = []
    for i, at in entry.items():
        specs[i] = pl.BlockSpec(memory_space=pltpu.HBM)
        extra.append(pltpu.VMEM(ins[i].shape if at is None else ins[i].shape[1:], ins[i].dtype))

    def outer(*refs):
        sems = refs[-1]
        held = refs[len(refs) - 1 - len(entry) : -1]
        refs = list(refs[: len(refs) - 1 - len(entry)])
        copies = []
        for n, (i, at) in enumerate(entry.items()):
            source = refs[i] if at is None else refs[i].at[at]
            copies.append(pltpu.make_async_copy(source, held[n], sems.at[n]))
            refs[i] = held[n]
        for copy in copies:
            copy.start()
        for copy in copies:
            copy.wait()
        body(*refs)

    return outer, [*scratch, *extra, pltpu.SemaphoreType.DMA((len(entry),))]


def ordered_slots(y, order, ref, outs):
    ones = jnp.ones((8, DH), BF16)
    squares = jnp.zeros((8, SEG), F32)
    for s in range(4):
        x = nn(order, ref[:, slab((y + s) % 4)])
        if outs is not None:
            outs[s][...] = x.astype(BF16)
        square = x * x
        high = square.astype(BF16)
        low = (square - high.astype(F32)).astype(BF16)
        squares = squares + nt(ones, high) + nt(ones, low)
    return squares


def prep_v_kernel(ids, v, o0, o1, o2, o3):
    order = order_matrix(False)
    for s, out in enumerate((o0, o1, o2, o3)):
        out[...] = nn(order, v[:, slab((ids[1] + s) % 4)]).astype(BF16)


def prep_k_kernel(ids, k, q, o0, o1, o2, o3, stats_out):
    order = order_matrix(False)
    key_sums = ordered_slots(ids[1], order, k, (o0, o1, o2, o3))
    query_sums = ordered_slots(ids[1], order, q, None)
    both = jnp.concatenate([query_sums[0:1], key_sums[0:1]], axis=0)
    for i in range(32):
        stats_out[i] = both


def prep_qg_kernel(ids, q, g, o0, o1, o2, o3):
    order = order_matrix(False)
    for s, out in enumerate((o0, o1, o2, o3)):
        at = slab((ids[1] + s) % 4)
        out[0] = nn(order, q[:, at]).astype(BF16)
        out[1] = nn(order, g[:, at]).astype(BF16)


def total_rows(ref, first, count, which):
    total = ref[first, which : which + 1]
    for i in range(1, count):
        total = total + ref[first + i, which : which + 1]
    return total


def inverse_row(stats, c, which):
    return lax.rsqrt(total_rows(stats, 8 * c, 8, which) / D + EPSILON)


def normed(raw, inverse, gain):
    t = jnp.transpose(raw.astype(F32)) * inverse * gain
    return jnp.transpose(t).astype(BF16)


def place_v_kernel(ids, p0, p1, p2, p3, out):
    y = ids[1]
    for s, piece in enumerate((p0, p1, p2, p3)):
        out[(y + 4 - s) % 4] = piece[...].reshape(4, 128, DH)


def gain_column(ids, gain):
    row = gain[:, slab(ids[1])].astype(F32)
    return jnp.transpose(jnp.broadcast_to(row, (DH, DH)))[:, 0:1]


def norm_k_kernel(ids, p0, p1, p2, p3, stats, gain, out):
    y = ids[1]
    scale = gain_column(ids, gain)
    for s, piece in enumerate((p0, p1, p2, p3)):
        c = (y + 4 - s) % 4
        out[c] = normed(piece[...], inverse_row(stats, c, 1), scale).reshape(4, 128, DH)


def head_bits(ids):
    h = 4 * ids[2] + ids[1]
    par = h & 1
    return par, 2 * par + ((h >> 1) & 1), (h >> 2) & 1


def forward_part(keys, vals, q, score_ref, mask=None, keep=False):
    count = len(keys)
    top = None
    for j in range(count):
        s = nt(keys[j](), q) * SCALE
        score_ref[j] = s
        t = jnp.max(s, axis=0, keepdims=True)
        top = t if top is None else jnp.maximum(top, t)
    if mask is not None:
        top = jnp.where(mask, top, FLOOR)
    total, summed = None, None
    for j in range(count):
        w = jnp.exp(score_ref[j] - top)
        if mask is not None:
            w = jnp.where(mask, w, 0.0)
        if keep:
            score_ref[j] = w
        t = jnp.sum(w, axis=0, keepdims=True)
        a = tn(vals[j](), w.astype(BF16))
        total = t if total is None else total + t
        summed = a if summed is None else summed + a
    return top, total, summed


def merge(m_ref, l_ref, a_ref, at, top, total, summed):
    m = m_ref[at]
    new = jnp.maximum(m, top)
    old_f = jnp.exp(m - new)
    new_f = jnp.exp(top - new)
    m_ref[at] = new
    l_ref[at] = old_f * l_ref[at] + new_f * total
    a_ref[at] = old_f * a_ref[at] + new_f * summed


def cut(x, b):
    return x[:, b * 128 : (b + 1) * 128]


def rows_of(ref, spots):
    return jnp.concatenate([ref[c, b] for c, b in spots], axis=0)


def chunks_of(ref, spots):
    return [lambda at=spots[i : i + PER]: rows_of(ref, at) for i in range(0, len(spots), PER)]


def level_forward_kernel(ids, p0, p1, p2, p3, stats, gain, k, v, q, g, m_out, l_out, a_out, score):
    y = ids[1]
    par, quarter, _ = head_bits(ids)
    scale = gain_column(ids, gain)
    for s, piece in enumerate((p0, p1, p2, p3)):
        c = (y + 4 - s) % 4
        q[c] = normed(piece[0], inverse_row(stats, c, 0), scale).reshape(4, 128, DH)
        g[c] = piece[1].reshape(4, 128, DH)

    def level0(c, carry):
        spots = [(c, b) for b in range(4)]
        top, total, summed = forward_part(
            chunks_of(k, spots), chunks_of(v, spots), rows_of(q, spots), score
        )
        for b in range(4):
            m_out[c, b] = cut(top, b)
            l_out[c, b] = cut(total, b)
            a_out[c, b] = cut(summed, b)
        return carry

    lax.fori_loop(0, 4, level0, 0)

    def joined(spots):
        top, total, summed = forward_part(
            chunks_of(k, spots), chunks_of(v, spots), rows_of(q, spots), score
        )
        for i, at in enumerate(spots):
            merge(m_out, l_out, a_out, at, cut(top, i), cut(total, i), cut(summed, i))

    def level1(s, carry):
        joined([(2 * s + i // 2, 2 * par + i % 2) for i in range(4)])
        return carry

    lax.fori_loop(0, 2, level1, 0)
    joined([(i, quarter) for i in range(4)])


def backward_chunk(key, val, q, g, lse, delta, mask=None):
    soft = jnp.exp(nt(key, q) * SCALE - lse)
    if mask is not None:
        soft = jnp.where(mask, soft, 0.0)
    grad = (soft * (nt(val, g) - delta)).astype(BF16)
    return tn(key, grad), nn(grad, q) * SCALE, nn(soft.astype(BF16), g)


def place(ids, lists, c, j):
    block = lists[j, 4 * ids[0] + c]
    owner = block // 4
    return ((owner // 4) + 4 - ids[0]) % 4, owner % 4, block % 4


def runs(lb):
    return [(rb // 2, pl.ds(pl.multiple_of((rb % 2) * 64 + lb * 16, 16), 16)) for rb in range(8)]


def level3_spots(ids):
    _, quarter, half = head_bits(ids)
    halves = pl.ds(pl.multiple_of(half * 64, 64), 64)
    mask = (lax.broadcasted_iota(jnp.int32, (1, SEG), 1) % 128) // 64 == half
    partner = jnp.where(ids[0] % 2 == 0, 1, 3)
    return quarter, halves, mask, partner


def quarter_row(ref, c, quarter):
    out = cut(ref[c], 0)
    for i in range(1, 4):
        out = jnp.where(quarter == i, cut(ref[c], i), out)
    return out


def kept_part(w, factor, key, val, q, g, delta):
    soft = w * factor
    grad = (soft * (nt(val, g) - delta)).astype(BF16)
    return tn(key, grad), nn(grad, q) * SCALE, nn(soft.astype(BF16), g)


def main_kernel(
    ids, lists, q, g, k0, v0, k1, v1, k2a, k2b, v2a, v2b, k3, v3, m_in, l_in, a_in,
    att, dq, lse_out, delta_out, dk_own, dv_own, v_up, v_down, k_up, k_down, vp, vn, kp, kn,
    kall, vall, dk, dv, score, score3, m, l, a, sems,
):
    quarter, halves, mask, partner = level3_spots(ids)
    copies = []
    for n, (dst, group) in enumerate(((kall, (k0, k1, k2a, k2b, k3)), (vall, (v0, v1, v2a, v2b, v3)))):
        places = (dst.at[0], dst.at[1], dst.at[2, 0:2], dst.at[2, 2:4], dst.at[3])
        for i, (src, to) in enumerate(zip(group, places)):
            copies.append(pltpu.make_async_copy(src, to, sems.at[n, i]))
    for copy in copies:
        copy.start()
    m[...] = m_in[...]
    l[...] = l_in[...]
    a[...] = a_in[...]
    dk[...] = jnp.zeros(dk.shape, F32)
    dv[...] = jnp.zeros(dv.shape, F32)
    for copy in copies:
        copy.wait()

    spots3 = [(at, c, quarter, halves) for at in (0, partner) for c in range(4)]
    rows3 = [(c, quarter) for c in range(4)]

    def eight(ref):
        return jnp.concatenate([ref[at] for at in spots3], axis=0)

    top3, total, summed = forward_part(
        [lambda: eight(kall)], [lambda: eight(vall)], rows_of(q, rows3), score3, mask, True
    )
    for i in range(4):
        merge(m, l, a, (i, quarter), cut(top3, i), cut(total, i), cut(summed, i))

    def one_ctx(c, carry):
        rows = q[c].reshape(SEG, DH)
        grows = g[c].reshape(SEG, DH)
        groups = []
        for i in (0, 4):
            spots = []
            for j in range(i, i + 4):
                rel, cc, lb = place(ids, lists, c, j)
                spots += [(rel, cc, b, r) for b, r in runs(lb)]
            groups.append(spots)

        def blocks(ref):
            return [lambda at=at: jnp.concatenate([ref[x] for x in at], axis=0) for at in groups]

        keys, vals = blocks(kall), blocks(vall)
        top, total, summed = forward_part(keys, vals, rows, score, None, True)
        for b in range(4):
            merge(m, l, a, (c, b), cut(top, b), cut(total, b), cut(summed, b))
        joint = jnp.concatenate([m[c, b] for b in range(4)], axis=1)
        whole = jnp.concatenate([l[c, b] for b in range(4)], axis=1)
        merged = jnp.concatenate([a[c, b] for b in range(4)], axis=1) / whole
        att[c] = merged.astype(BF16)
        lse = joint + jnp.log(whole)
        delta = jnp.sum(jnp.transpose(grows.astype(F32)) * merged, axis=0, keepdims=True)
        lse_out[c] = lse
        delta_out[c] = delta
        factor = jnp.exp(top - lse)
        grad_q = None
        for n, spots in enumerate(groups):
            gq, gk, gv = kept_part(score[n], factor, keys[n](), vals[n](), rows, grows, delta)
            grad_q = gq if grad_q is None else grad_q + gq
            gk = gk.astype(BF16).astype(F32)
            gv = gv.astype(BF16).astype(F32)
            for i, spot in enumerate(spots):
                dk[spot] = dk[spot] + gk[16 * i : 16 * (i + 1)]
                dv[spot] = dv[spot] + gv[16 * i : 16 * (i + 1)]
        for b in range(4):
            dq[c, b] = cut(grad_q, b) * SCALE
        return carry

    lax.fori_loop(0, 4, one_ctx, 0)
    logs = jnp.concatenate([quarter_row(lse_out, c, quarter) for c in range(4)], axis=1)
    deltas = jnp.concatenate([quarter_row(delta_out, c, quarter) for c in range(4)], axis=1)
    gq, gk, gv = kept_part(
        score3[0], jnp.exp(top3 - logs), eight(kall), eight(vall), rows_of(q, rows3), rows_of(g, rows3), deltas
    )
    for c in range(4):
        dq[c, quarter] = dq[c, quarter] + cut(gq, c) * SCALE
    for n, spot in enumerate(spots3):
        dk[spot] = dk[spot] + gk[64 * n : 64 * (n + 1)]
        dv[spot] = dv[spot] + gv[64 * n : 64 * (n + 1)]
    dk_own[...] = dk[0]
    dv_own[...] = dv[0]
    for ref, up, down, up_kept, down_kept in ((dv, v_up, v_down, vp, vn), (dk, k_up, k_down, kp, kn)):
        up[0] = ref[2, 0:2].astype(BF16)
        up[1] = ref[1, 2:4].astype(BF16)
        down[0] = ref[2, 2:4].astype(BF16)
        down[1] = ref[3, 0:2].astype(BF16)
        up_kept[...] = ref[1, 0:2]
        down_kept[...] = ref[3, 2:4]


def relay_kernel(up, down, from_below, from_above, up_out, down_out):
    up_out[...] = (up[...] + from_below[...].astype(F32)).astype(BF16)
    down_out[...] = (down[...] + from_above[...].astype(F32)).astype(BF16)


def put_pair(out, x):
    high = x.astype(BF16)
    out[0] = high
    out[1] = (x - high.astype(F32)).astype(BF16)


def main3_kernel(
    ids, q, g, k, v, lse, delta, dq_in, dk_in, dv_in, p0, p1, p2, p3, gain, att,
    dk, dv, a0, a1, a2, a3, s_out, dq,
):
    y = ids[1]
    par, quarter, _ = head_bits(ids)
    dq[...] = dq_in[...]
    dk[...] = dk_in[...]
    dv[...] = dv_in[...]

    def part(spots, rows, grows, logs, deltas):
        for i in range(0, 4, PER):
            at = spots[i : i + PER]
            gq, gk, gv = backward_chunk(rows_of(k, at), rows_of(v, at), rows, grows, logs, deltas)
            for n, (c, b) in enumerate(at):
                dk[c, b] = dk[c, b] + gk[128 * n : 128 * (n + 1)]
                dv[c, b] = dv[c, b] + gv[128 * n : 128 * (n + 1)]
            for n, (c, b) in enumerate(spots):
                dq[c, b] = dq[c, b] + cut(gq, n) * SCALE

    def gather(spots):
        return (
            rows_of(q, spots),
            rows_of(g, spots),
            jnp.concatenate([quarter_row(lse, c, b) for c, b in spots], axis=1),
            jnp.concatenate([quarter_row(delta, c, b) for c, b in spots], axis=1),
        )

    def level0(c, carry):
        part([(c, b) for b in range(4)], q[c].reshape(SEG, DH), g[c].reshape(SEG, DH), lse[c], delta[c])
        return carry

    lax.fori_loop(0, 4, level0, 0)

    def level1(s, carry):
        spots = [(2 * s + i // 2, 2 * par + i % 2) for i in range(4)]
        part(spots, *gather(spots))
        return carry

    lax.fori_loop(0, 2, level1, 0)
    spots = [(i, quarter) for i in range(4)]
    part(spots, *gather(spots))
    pieces = (p0, p1, p2, p3)
    scale = gain_column(ids, gain)
    for s, out in enumerate((a0, a1, a2, a3)):
        c = (y + s) % 4
        raw = jnp.transpose(pieces[(4 - s) % 4][0].astype(F32))
        adj = jnp.concatenate([dq[c, b] for b in range(4)], axis=1) * scale
        put_pair(out, adj)
        out[2] = att[c]
        s_out[c] = jnp.sum(raw * adj, axis=0, keepdims=True)


def add_rows(own, below1, above1, below2, above2, total):
    total[0:2] = own[0:2] + below2[...].astype(F32) + above1[...].astype(F32)
    total[2:4] = own[2:4] + below1[...].astype(F32) + above2[...].astype(F32)


def collect_v_kernel(ids, dv, below1, above1, below2, above2, o0, o1, o2, o3, total):
    add_rows(dv, below1, above1, below2, above2, total)
    for s, out in enumerate((o0, o1, o2, o3)):
        out[...] = jnp.transpose(total[(ids[1] + s) % 4].reshape(SEG, DH)).astype(BF16)


def collect_k_kernel(
    ids, dk, below1, above1, below2, above2, p0, p1, p2, p3, gain, q_inner,
    o0, o1, o2, o3, s_out, total,
):
    add_rows(dk, below1, above1, below2, above2, total)
    pieces = (p0, p1, p2, p3)
    scale = gain_column(ids, gain)
    for s, out in enumerate((o0, o1, o2, o3)):
        c = (ids[1] + s) % 4
        raw = jnp.transpose(pieces[(4 - s) % 4][...].astype(F32))
        adj = jnp.transpose(total[c].reshape(SEG, DH)) * scale
        put_pair(out, adj)
        inner = jnp.concatenate([q_inner[c], jnp.sum(raw * adj, axis=0, keepdims=True)], axis=0)
        for h in range(8):
            s_out[8 * c + h] = inner


def restore_kernel(ids, p0, p1, p2, p3, out):
    y = ids[1]
    order = order_matrix(True)
    for s, piece in enumerate((p0, p1, p2, p3)):
        out[:, slab((y + 4 - s) % 4)] = nt(order, piece[...]).astype(BF16)


def ready_q_kernel(ids, stats, raw, p0, p1, p2, p3, first, second, plain):
    y = ids[1]
    order = order_matrix(True)
    r = inverse_row(stats, y, 0)
    for s, piece in enumerate((p0, p1, p2, p3)):
        at = slab((y + 4 - s) % 4)
        first[s] = r * (piece[0].astype(F32) + piece[1].astype(F32))
        second[s] = tn(raw[:, at], order) * (r * r * r)
        plain[:, at] = nt(order, piece[2]).astype(BF16)


def finish_kernel(ids, inner, stats, first, second, raw, p0, p1, p2, p3, q_out, k_out):
    y = ids[1]
    order = order_matrix(True)
    total = total_rows(inner, 0, 32, 0) / D
    for s in range(4):
        grads = (first[s] - second[s] * total).astype(BF16)
        q_out[:, slab((y + 4 - s) % 4)] = nt(order, grads).astype(BF16)
    total = total_rows(inner, 0, 32, 1) / D
    r = inverse_row(stats, y, 1)
    for s, piece in enumerate((p0, p1, p2, p3)):
        at = slab((y + 4 - s) % 4)
        x = tn(raw[:, at], order)
        adj = piece[0].astype(F32) + piece[1].astype(F32)
        grads = (r * adj - x * (r * r * r) * total).astype(BF16)
        k_out[:, at] = nt(order, grads).astype(BF16)


def shift(value, axis, step):
    return lax.ppermute(value, axis, [(i, (i + step) % 4) for i in range(4)])


def y_exchange(slots):
    far = shift(slots[2], "y", 2)
    return [slots[0], shift(slots[1], "y", 1), far, shift(slots[3], "y", -1)]


def to_all(copies):
    return lax.all_to_all(copies, ("y", "head"), split_axis=0, concat_axis=0, tiled=True)


def shards_inner(queries, key_states, values, query_gain, key_gain, memory_blocks, cotangent):
    z, y, hd = lax.axis_index("z"), lax.axis_index("y"), lax.axis_index("head")
    ids = jnp.stack([z, y, hd]).astype(jnp.int32)

    q_gain, k_gain = query_gain.reshape(1, 4 * DH), key_gain.reshape(1, 4 * DH)
    lists = memory_blocks.T
    head4 = (4, 4, 128, DH)
    one, full = S(head4, BF16), S(head4, F32)
    slot = S((2, SEG, DH), BF16)
    back = S((3, DH, SEG), BF16)
    row, row4 = S((4, 1, SEG), F32), S((4, 4, 1, 128), F32)
    flat = S((SEG, 4 * DH), BF16)

    part = S((SEG, DH), BF16)
    v_slots = call(prep_v_kernel, (ids, values), 1, (part,) * 4)
    v_pieces = y_exchange(v_slots)
    *k_slots, sums = call(
        prep_k_kernel, (ids, key_states, queries), 1, (part,) * 4 + (S((32, 2, SEG), F32),)
    )
    k_pieces = y_exchange(k_slots)
    stats = to_all(sums)
    qg = call(prep_qg_kernel, (ids, queries, cotangent), 1, (slot,) * 4)
    qg_pieces = y_exchange(qg)
    v0 = call(place_v_kernel, (ids, *v_pieces), 1, one)
    v3, v1 = shift(v0, "z", 1), shift(v0, "z", -1)
    k0 = call(norm_k_kernel, (ids, *k_pieces, stats, k_gain), 1, one)
    k3, k1 = shift(k0, "z", 1), shift(k0, "z", -1)
    v2a, v2b = shift(v3[0:2], "z", 1), shift(v1[2:4], "z", -1)
    k2a, k2b = shift(k3[0:2], "z", 1), shift(k1[2:4], "z", -1)
    q, g, m, l, a = call(
        level_forward_kernel,
        (ids, *qg_pieces, stats, q_gain, k0, v0),
        1,
        (one, one, row4, row4, full),
        [pltpu.VMEM((4 // PER, 128 * PER, SEG), F32)],
        flops=7 * 2 * 2 * 512 * 512 * 128,
    )
    half, kept = S((2, 2, 4, 128, DH), BF16), S((2, 4, 128, DH), F32)
    att, dq, lse, delta, dk, dv, v_up, v_down, k_up, k_down, vp, vn, kp, kn = call(
        main_kernel,
        (ids, lists, q, g, k0, v0, k1, v1, k2a, k2b, v2a, v2b, k3, v3, m, l, a),
        2,
        (S((4, DH, SEG), BF16), full, row, row, full, full) + (half,) * 4 + (kept,) * 4,
        [
            pltpu.VMEM((4, *head4), BF16),
            pltpu.VMEM((4, *head4), BF16),
            pltpu.VMEM((4, *head4), F32),
            pltpu.VMEM((4, *head4), F32),
            pltpu.VMEM((2, SEG, SEG), F32),
            pltpu.VMEM((1, SEG, SEG), F32),
            pltpu.VMEM((4, 4, 1, 128), F32),
            pltpu.VMEM((4, 4, 1, 128), F32),
            pltpu.VMEM(head4, F32),
            pltpu.SemaphoreType.DMA((2, 5)),
        ],
        flops=9 * 6 * 2 * 512 * 512 * 128,
        far=range(4, 14),
        room=30,
    )
    v_below, v_above = shift(v_up, "z", 1), shift(v_down, "z", -1)
    k_below, k_above = shift(k_up, "z", 1), shift(k_down, "z", -1)
    dk, dv, *q_slots, q_s = call(
        main3_kernel,
        (ids, q, g, k0, v0, lse, delta, dq, dk, dv, *qg_pieces, q_gain, att),
        1,
        (full, full) + (back,) * 4 + (row,),
        [pltpu.VMEM(head4, F32)],
        flops=7 * 5 * 2 * 512 * 512 * 128,
    )

    def relayed(up, down, below, above):
        pair = S((2, 4, 128, DH), BF16)
        return call(relay_kernel, (up, down, below, above), 0, (pair, pair), fetch={2: 0, 3: 0})

    v_up, v_down = relayed(vp, vn, v_below, v_above)
    v_below2, v_above2 = shift(v_up, "z", 1), shift(v_down, "z", -1)
    k_up, k_down = relayed(kp, kn, k_below, k_above)
    k_below2, k_above2 = shift(k_up, "z", 1), shift(k_down, "z", -1)
    q_adj = y_exchange(q_slots)
    v_slots = call(
        collect_v_kernel,
        (ids, dv, v_below, v_above, v_below2, v_above2),
        1,
        (S((DH, SEG), BF16),) * 4,
        [pltpu.VMEM(head4, F32)],
        fetch={2: 1, 3: 1},
    )
    v_back = y_exchange(v_slots)
    value_grads = call(restore_kernel, (ids, *v_back), 1, flat)
    *k_slots, inner = call(
        collect_k_kernel,
        (ids, dk, k_below, k_above, k_below2, k_above2, *k_pieces, k_gain, q_s),
        1,
        (S((2, DH, SEG), BF16),) * 4 + (S((32, 2, SEG), F32),),
        [pltpu.VMEM(head4, F32)],
        fetch={2: 1, 3: 1},
    )
    k_adj = y_exchange(k_slots)
    inner = to_all(inner)
    first, second, attended = call(
        ready_q_kernel,
        (ids, stats, queries, *q_adj),
        1,
        (S((4, DH, SEG), F32), S((4, DH, SEG), F32), flat),
    )
    query_grads, key_grads = call(
        finish_kernel, (ids, inner, stats, first, second, key_states, *k_adj), 1, (flat, flat)
    )
    return (attended, query_grads, key_grads, value_grads)


PER = 4


def solution(mesh):
    split = Mesh(mesh.devices.reshape(4, 4, 8), ("z", "y", "head"))
    big = P(("z", "y"), "head")
    in_specs = (big, big, big, P("head"), P("head"), P(), big)
    return jax.shard_map(
        shards_inner, mesh=split, in_specs=in_specs, out_specs=(big, big, big, big), check_vma=False
    )
```
